32 devices in a mesh: ctx: 16 (over z, y, core), shard: 2 (over x).
Axes of the slice: x: 2, y: 2, z: 4, core: 2. Of those that a mesh axis runs over, the one named last changes fastest.
Arguments:
- query: bfloat16 [4096, 2048], P('ctx', 'shard'), may hold values from -6 to 6
- key: bfloat16 [4096, 1024], P('ctx', 'shard'), may hold values from -6 to 6
- value: bfloat16 [4096, 1024], P('ctx', 'shard'), may hold values from -6 to 6
- attention_output: bfloat16 [4096, 2048], P('ctx', 'shard'), may hold values from -3 to 3
- grad_y: bfloat16 [4096, 2048], P('ctx'), may hold values from -24 to 24
- doc_ids: int32 [4096], P('ctx'), may hold values from 0 to 7, never falling along the last dimension, each value on 1 to 1024 neighbouring positions
- codes: bfloat16 [2048, 2048], P('shard', 'ctx'), may hold values from -0.125 to 0.125
- scale_copies: float32 [2, 16, 128], P('shard'), may hold values from 0.5 to 2
- holder: int32 [16], replicated, may hold values from 0 to 1
Outputs:
- grad_query: bfloat16 [4096, 2048], P('ctx', 'shard')
- key_gradient: bfloat16 [4096, 1024], P('ctx', 'shard')
- value_gradient: bfloat16 [4096, 1024], P('ctx', 'shard')
- grad_weight: float32 [2048, 2048], P('ctx', 'shard')
The draws below stay inside these ranges and needn't reach their ends.
Inputs may be any that keep to these rules, and one draw needn't show every extreme that they name: doc_ids never falls along the sequence; each document holds 1 to 1024 positions, one exactly 1024. Only scale_copies[holder[p], p] is used for panel p.
All inputs are finite; a program needn't handle non-finite values.
Results may differ from the reference program's by a relative error of at most 0.008.
Values may be sent and summed in bfloat16 or wider, within the bound.
A program may use at most 64 MiB of HBM per device.

```python
import math
import jax
import jax.numpy as jnp
import numpy as np
from jax import lax

HEAD_WIDTH = 128
QUERY_HEADS = 16
KEY_VALUE_HEADS = 8
D_OUT = 2048
DOCS = 8
SEQUENCE_LENGTH = 4096
DOC_MOST = 1024
N_SHARD = 2


def drawn_pair(key):
    pairing_count = QUERY_HEADS // KEY_VALUE_HEADS
    starting_keys = jnp.clip(jax.random.normal(jax.random.fold_in(key, 11), (SEQUENCE_LENGTH, KEY_VALUE_HEADS, HEAD_WIDTH), jnp.float32), -5.0, 5.0)
    starting_query = jnp.clip(jax.random.normal(jax.random.fold_in(key, 12), (SEQUENCE_LENGTH, KEY_VALUE_HEADS, pairing_count, HEAD_WIDTH), jnp.float32), -5.0, 5.0)
    return (starting_query.reshape(SEQUENCE_LENGTH, QUERY_HEADS * HEAD_WIDTH), starting_keys.reshape(SEQUENCE_LENGTH, KEY_VALUE_HEADS * HEAD_WIDTH))


def draw_query(key, part):
    return drawn_pair(key)[0].astype(jnp.bfloat16)


def draw_key(key, part):
    return drawn_pair(key)[1].astype(jnp.bfloat16)


def place_ends(result, stream_key, low, high):
    index_at = [jax.random.randint(jax.random.fold_in(stream_key, axis), (), 0, length) for axis, length in enumerate(result.shape)]
    main_axis = result.shape.index(max(result.shape))
    neighbour = index_at[:main_axis] + [(index_at[main_axis] + 1) % result.shape[main_axis]] + index_at[main_axis + 1:]
    return result.at[tuple(index_at)].set(low).at[tuple(neighbour)].set(high)


def raised(result, stream_key, source, target, shards_of, factor):
    owner, partner = [(jnp.arange(result.shape[dim]) // (result.shape[dim] // shards_of)).reshape([-1 if axis == dim else 1 for axis in range(result.ndim)]) for dim in (source, target)]
    chosen = jax.random.permutation(stream_key, shards_of)[partner]
    strong = (owner == chosen) | (owner == (partner + shards_of // 2) % shards_of)
    return jnp.where(strong, factor * result, result)


def block_scale(key, shape, shards, least, high):
    loudness, own = 1.0, jax.random.fold_in(key, 6)
    for axis_at, shards_of in shards:
        draws = jnp.exp(jax.random.uniform(jax.random.fold_in(own, axis_at), (shards_of,), jnp.float32, least / len(shards), high / len(shards)))
        loudness = loudness * jnp.repeat(draws, shape[axis_at] // shards_of).reshape([-1 if axis == axis_at else 1 for axis in range(len(shape))])
    return loudness


def length_profile(number_of, total, bound, lean):
    portions = [(1 << 20) // math.isqrt(grade ** lean) + 1 for grade in range(2, number_of + 1)]
    spare, given = total - bound - (number_of - 1), [1] * (number_of - 1)
    while spare > 0:
        free = [i for i in range(number_of - 1) if given[i] < bound]
        whole, remaining = sum([portions[i] for i in free]), spare
        for i in free:
            more = min(bound - given[i], max(1, remaining * portions[i] // whole), spare)
            given[i] = given[i] + more
            spare = spare - more
    return np.array([bound] + given)


def ragged(key, amount, total, most, skew):
    if amount == 2:
        one = jax.random.randint(key, (), max(1, total - most), min(most, total - 1) + 1)
        return jnp.stack([one, total - one])
    tallies = jnp.asarray(length_profile(amount, total, most, skew), jnp.int32)
    couples = (amount - 1) // 2
    donor, sink = tallies[1:1 + 2 * couples:2], tallies[2:2 + 2 * couples:2]
    slack = jnp.minimum(donor - 1, most - sink)
    shifted = jax.random.randint(jax.random.fold_in(key, 1), (couples,), 0, 1 << 20) % (slack + 1)
    tallies = tallies.at[1:1 + 2 * couples:2].set(donor - shifted).at[2:2 + 2 * couples:2].set(sink + shifted)
    return tallies[jax.random.permutation(jax.random.fold_in(key, 2), amount)]


def gaussian(key, dims, scale, reach, split=(), kind=jnp.bfloat16):
    values = scale * jax.random.normal(key, dims, jnp.float32)
    if split:
        values = values * block_scale(key, dims, split, -0.22, 0.18)
    return jnp.clip(values, -reach, reach).astype(kind)


def bell_draw_with(key, dims, width, reach, shards, heavy, kind=jnp.bfloat16):
    array = width * jax.random.normal(key, dims, jnp.float32)
    if shards:
        array = array * block_scale(key, dims, shards, -0.22, 0.18)
    return jnp.clip(raised(array, jax.random.fold_in(key, 3), *heavy), -reach, reach).astype(kind)


def setup_inputs(seed: int = 0) -> dict:
    arg_keys = jax.random.split(jax.random.key(seed), 10)
    return {
        "query": draw_query(jax.random.fold_in(arg_keys[9], 71), 0),
        "key": draw_key(jax.random.fold_in(arg_keys[9], 71), 0),
        "value": gaussian(arg_keys[2], (SEQUENCE_LENGTH, KEY_VALUE_HEADS * HEAD_WIDTH), 1.0, 6.0, ((0, 16), (1, 2))),
        "attention_output": gaussian(arg_keys[3], (SEQUENCE_LENGTH, QUERY_HEADS * HEAD_WIDTH), 0.5, 3.0, ((0, 16), (1, 2))),
        "grad_y": bell_draw_with(arg_keys[4], (SEQUENCE_LENGTH, D_OUT), 4.0, 24.0, ((0, 16),), (0, 1, 16, 2.0)),
        "doc_ids": jnp.searchsorted(jnp.cumsum(ragged(arg_keys[5], DOCS, SEQUENCE_LENGTH, DOC_MOST, 0)), jnp.arange(SEQUENCE_LENGTH), side="right").astype(jnp.int32),
        "codes": gaussian(arg_keys[6], (QUERY_HEADS * HEAD_WIDTH, D_OUT), D_OUT ** -0.5, 0.125, ((0, 2), (1, 16))),
        "scale_copies": jnp.clip(jnp.exp(math.log(2.0) - 1.3862944 * jax.random.uniform(arg_keys[7], (N_SHARD, QUERY_HEADS, HEAD_WIDTH), jnp.float32) ** block_scale(arg_keys[7], (N_SHARD, QUERY_HEADS, HEAD_WIDTH), ((0, 2),), -0.2, 0.2)), 0.5, 2.0),
        "holder": place_ends(jax.random.randint(arg_keys[8], (QUERY_HEADS,), 0, N_SHARD), jax.random.fold_in(arg_keys[8], 1), 0, N_SHARD - 1).astype(jnp.int32),
    }


def group_grads(doc_ids, head_queries, head_keys, head_values, head_gradients, output_heads):
    block = min(512, SEQUENCE_LENGTH)
    blocks = SEQUENCE_LENGTH // block
    score_scale = HEAD_WIDTH ** -0.5
    pairing_count = head_queries.shape[0]
    row_delta = jnp.sum(head_gradients.astype(jnp.float32) * output_heads.astype(jnp.float32), axis=-1)
    offsets = jnp.arange(block, dtype=jnp.int32)

    def tile_mask(qb, kb):
        query_pos = qb * block + offsets
        key_pos = kb * block + offsets
        query_docs = lax.dynamic_slice_in_dim(doc_ids, qb * block, block)
        key_docs = lax.dynamic_slice_in_dim(doc_ids, kb * block, block)
        return (key_pos[None, :] <= query_pos[:, None]) & (key_docs[None, :] == query_docs[:, None])

    def tile_live(qb, kb):
        return (kb <= qb) & (doc_ids[kb * block + block - 1] >= doc_ids[qb * block])

    def row_stats(qb):
        qb = qb.astype(jnp.int32)
        query_rows = lax.dynamic_slice_in_dim(head_queries, qb * block, block, 1).astype(jnp.float32)

        def visit(kb, current):
            kb = kb.astype(jnp.int32)

            def live_branch(current):
                highest, running = current
                key_rows = lax.dynamic_slice_in_dim(head_keys, kb * block, block, 0).astype(jnp.float32)
                scores = jnp.einsum("jrd,nd->jrn", query_rows, key_rows) * score_scale
                allowed = tile_mask(qb, kb)[None]
                masked = jnp.where(allowed, scores, -1e30)
                newest = jnp.maximum(highest, jnp.max(masked, axis=-1))
                weights = jnp.where(allowed, jnp.exp(scores - newest[..., None]), 0.0)
                return newest, running * jnp.exp(highest - newest) + jnp.sum(weights, axis=-1)

            return lax.cond(tile_live(qb, kb), live_branch, lambda current: current, current)

        start = (jnp.full((pairing_count, block), -1e30, jnp.float32), jnp.zeros((pairing_count, block), jnp.float32))
        highest, running = lax.fori_loop(0, blocks, visit, start)
        return highest + jnp.log(running)

    log_total = lax.map(row_stats, jnp.arange(blocks, dtype=jnp.int32))
    log_total = log_total.transpose(1, 0, 2).reshape(pairing_count, SEQUENCE_LENGTH)

    def row_block(sums, qb):
        qb = qb.astype(jnp.int32)
        query_rows = lax.dynamic_slice_in_dim(head_queries, qb * block, block, 1).astype(jnp.float32)
        grad_rows = lax.dynamic_slice_in_dim(head_gradients, qb * block, block, 1).astype(jnp.float32)
        log_rows = lax.dynamic_slice_in_dim(log_total, qb * block, block, 1)
        delta_rows = lax.dynamic_slice_in_dim(row_delta, qb * block, block, 1)

        def visit(kb, loop_state):
            kb = kb.astype(jnp.int32)

            def live_branch(loop_state):
                query_grad, key_grad, value_grad = loop_state
                key_rows = lax.dynamic_slice_in_dim(head_keys, kb * block, block, 0).astype(jnp.float32)
                value_rows = lax.dynamic_slice_in_dim(head_values, kb * block, block, 0).astype(jnp.float32)
                scores = jnp.einsum("jrd,nd->jrn", query_rows, key_rows) * score_scale
                allowed = tile_mask(qb, kb)[None]
                attention = jnp.where(allowed, jnp.exp(scores - log_rows[..., None]), 0.0)
                attention_low = attention.astype(jnp.bfloat16).astype(jnp.float32)
                attention_grad = jnp.einsum("jrd,nd->jrn", grad_rows, value_rows)
                score_grad = (attention * (attention_grad - delta_rows[..., None])).astype(jnp.bfloat16).astype(jnp.float32)
                query_add = score_scale * jnp.einsum("jrn,nd->jrd", score_grad, key_rows)
                key_add = score_scale * jnp.einsum("jrn,jrd->nd", score_grad, query_rows)
                value_add = jnp.einsum("jrn,jrd->nd", attention_low, grad_rows)
                key_old = lax.dynamic_slice_in_dim(key_grad, kb * block, block, 0)
                value_old = lax.dynamic_slice_in_dim(value_grad, kb * block, block, 0)
                key_grad = lax.dynamic_update_slice_in_dim(key_grad, key_old + key_add, kb * block, 0)
                value_grad = lax.dynamic_update_slice_in_dim(value_grad, value_old + value_add, kb * block, 0)
                return query_grad + query_add, key_grad, value_grad

            return lax.cond(tile_live(qb, kb), live_branch, lambda loop_state: loop_state, loop_state)

        start = (jnp.zeros((pairing_count, block, HEAD_WIDTH), jnp.float32), sums[0], sums[1])
        query_grad, key_grad, value_grad = lax.fori_loop(0, blocks, visit, start)
        return (key_grad, value_grad), query_grad

    zeros_key = jnp.zeros((SEQUENCE_LENGTH, HEAD_WIDTH), jnp.float32)
    sums, query_grads = lax.scan(row_block, (zeros_key, zeros_key), jnp.arange(blocks, dtype=jnp.int32))
    query_grads = query_grads.transpose(1, 0, 2, 3).reshape(pairing_count, SEQUENCE_LENGTH, HEAD_WIDTH)
    return query_grads, sums[0], sums[1]


def reference(query, key, value, attention_output, grad_y, doc_ids, codes, scale_copies, holder):
    scale_table = scale_copies[holder, jnp.arange(QUERY_HEADS, dtype=jnp.int32)]
    row_scale = scale_table.reshape(QUERY_HEADS * HEAD_WIDTH)
    weight = (codes.astype(jnp.float32) * row_scale[:, None]).astype(jnp.bfloat16)
    attention_gradient = jnp.dot(grad_y, weight.T, preferred_element_type=jnp.float32).astype(jnp.bfloat16)
    grad_weight = jnp.dot(grad_y.T, attention_output, preferred_element_type=jnp.float32) * (SEQUENCE_LENGTH ** -0.5)
    pairing_count = QUERY_HEADS // KEY_VALUE_HEADS
    head_queries = query.reshape(SEQUENCE_LENGTH, KEY_VALUE_HEADS, pairing_count, HEAD_WIDTH).transpose(1, 2, 0, 3)
    head_gradients = attention_gradient.reshape(SEQUENCE_LENGTH, KEY_VALUE_HEADS, pairing_count, HEAD_WIDTH).transpose(1, 2, 0, 3)
    output_heads = attention_output.reshape(SEQUENCE_LENGTH, KEY_VALUE_HEADS, pairing_count, HEAD_WIDTH).transpose(1, 2, 0, 3)
    head_keys = key.reshape(SEQUENCE_LENGTH, KEY_VALUE_HEADS, HEAD_WIDTH).transpose(1, 0, 2)
    head_values = value.reshape(SEQUENCE_LENGTH, KEY_VALUE_HEADS, HEAD_WIDTH).transpose(1, 0, 2)

    def one_group(operands):
        return group_grads(doc_ids, operands[0], operands[1], operands[2], operands[3], operands[4])

    query_grads, key_gradient_list, value_gradient_list = lax.map(one_group, (head_queries, head_keys, head_values, head_gradients, output_heads))
    grad_query = query_grads.transpose(2, 0, 1, 3).reshape(SEQUENCE_LENGTH, QUERY_HEADS * HEAD_WIDTH).astype(jnp.bfloat16)
    key_gradient = key_gradient_list.transpose(1, 0, 2).reshape(SEQUENCE_LENGTH, KEY_VALUE_HEADS * HEAD_WIDTH).astype(jnp.bfloat16)
    value_gradient = value_gradient_list.transpose(1, 0, 2).reshape(SEQUENCE_LENGTH, KEY_VALUE_HEADS * HEAD_WIDTH).astype(jnp.bfloat16)
    return grad_query, key_gradient, value_gradient, grad_weight
```

```python
import functools
import jax
import jax.numpy as jnp
from jax import lax
from jax.experimental import pallas as pl
from jax.sharding import PartitionSpec as P

HEAD_WIDTH = 128
LOW = -1e30
LAST = (((1,), (1,)), ((), ()))
FIRST = (((0,), (0,)), ((), ()))
PLAIN = (((1,), (0,)), ((), ()))


def dot(a, b, dims):
    return lax.dot_general(a, b, dims, preferred_element_type=jnp.float32)


def stacked(ref, pairs):
    return jnp.concatenate(
        [ref[:, j * HEAD_WIDTH : (j + 1) * HEAD_WIDTH] for j in range(pairs)], axis=0
    )


def row_of(ref, pairs):
    return jnp.concatenate([ref[0, j : j + 1, :] for j in range(pairs)], axis=1)


def visible(key_docs_ref, query_docs_ref, pairs, own):
    key_docs = key_docs_ref[:, 0:1].astype(jnp.float32)
    query_docs = query_docs_ref[...]
    allowed = key_docs == query_docs
    if own:
        rows = query_docs.shape[1]
        n = lax.broadcasted_iota(jnp.int32, (rows, rows), 0)
        r = lax.broadcasted_iota(jnp.int32, (rows, rows), 1)
        allowed = allowed & (n <= r)
    return jnp.concatenate([allowed.astype(jnp.float32)] * pairs, axis=1) > 0.5


def stats_kernel(own, final, pairs, scale, q_ref, k_ref, kd_ref, qd_ref, m_ref, l_ref, *outs):
    rows = q_ref.shape[0]
    scores = dot(k_ref[...], stacked(q_ref, pairs), LAST) * scale
    allowed = visible(kd_ref, qd_ref, pairs, own)
    masked = jnp.where(allowed, scores, LOW)
    highest, running = row_of(m_ref, pairs), row_of(l_ref, pairs)
    newest = jnp.maximum(highest, jnp.max(masked, axis=0, keepdims=True))
    weights = jnp.where(allowed, jnp.exp(scores - newest), 0.0)
    total = running * jnp.exp(highest - newest) + jnp.sum(weights, axis=0, keepdims=True)
    results = (newest + jnp.log(total),) if final else (newest, total)
    for out, result in zip(outs, results):
        for j in range(pairs):
            out[0, j : j + 1, :] = result[:, j * rows : (j + 1) * rows]


def grads_kernel(
    own, first, pairs, scale, q_ref, a_ref, k_ref, v_ref, kd_ref, qd_ref, t_ref, d_ref, *rest
):
    if first:
        dq_ref, kv_ref = rest
    else:
        old_ref, dq_ref, kv_ref = rest
    rows = q_ref.shape[0]
    queries, grads = stacked(q_ref, pairs), stacked(a_ref, pairs)
    keys, values = k_ref[...], v_ref[...]
    scores = dot(keys, queries, LAST) * scale
    allowed = visible(kd_ref, qd_ref, pairs, own)
    attention = jnp.where(allowed, jnp.exp(scores - row_of(t_ref, pairs)), 0.0)
    attention_grad = dot(values, grads, LAST)
    score_grad = (attention * (attention_grad - row_of(d_ref, pairs))).astype(jnp.bfloat16)
    kv_ref[0] = (dot(score_grad, queries, PLAIN) * scale).astype(kv_ref.dtype)
    kv_ref[1] = dot(attention.astype(jnp.bfloat16), grads, PLAIN).astype(kv_ref.dtype)
    query_add = dot(score_grad, keys, FIRST) * scale
    for j in range(pairs):
        part = query_add[j * rows : (j + 1) * rows, :]
        cols = slice(j * HEAD_WIDTH, (j + 1) * HEAD_WIDTH)
        if not first:
            part = part + old_ref[:, cols]
        dq_ref[:, cols] = part.astype(dq_ref.dtype)


def shift_by(x, axis, by):
    size = lax.axis_size(axis)
    return lax.ppermute(x, axis, [(i, i + by) for i in range(size) if 0 <= i + by < size])


def per_device(query, key, value, attention_output, grad_y, doc_ids, codes, scale_copies, holder):
    rows = query.shape[0]
    heads = query.shape[1] // HEAD_WIDTH
    groups = key.shape[1] // HEAD_WIDTH
    pairs = heads // groups
    shard_index = lax.axis_index("shard")
    shards = lax.axis_size("shard")
    ctx_count = lax.axis_size("ctx")
    steps = ctx_count // 4 + 1
    scale = HEAD_WIDTH ** (-0.5)

    gathered = lax.all_gather(codes, "ctx", axis=1, tiled=True)

    docs = (doc_ids + 1).astype(jnp.bfloat16)
    packed = jnp.concatenate(
        [key, value, jnp.broadcast_to(docs[:, None], (rows, HEAD_WIDTH))], axis=1
    )
    query_docs = (doc_ids + 1).astype(jnp.float32)[None, :]
    blocks = [packed] + [shift_by(packed, "ctx", d) for d in range(1, steps)]

    masked_table = jnp.where((holder == shard_index)[:, None], scale_copies[0], 0.0)
    scale_table = masked_table
    for i in range(1, shards):
        scale_table = scale_table + lax.ppermute(
            masked_table, "shard", [(j, (j + i) % shards) for j in range(shards)]
        )
    row_scale = lax.dynamic_slice_in_dim(scale_table, shard_index * heads, heads, 0).reshape(
        heads * HEAD_WIDTH
    )

    partial_weight = (
        dot(grad_y, attention_output, FIRST) * (rows * ctx_count) ** (-0.5)
    ).astype(jnp.bfloat16)
    scattered = lax.psum_scatter(partial_weight, "ctx", scatter_dimension=0, tiled=True)

    pair_spec = pl.BlockSpec((rows, pairs * HEAD_WIDTH), lambda g: (0, g))
    key_spec = pl.BlockSpec((rows, HEAD_WIDTH), lambda g: (0, g))
    value_spec = pl.BlockSpec((rows, HEAD_WIDTH), lambda g: (0, groups + g))
    docs_spec = pl.BlockSpec((rows, HEAD_WIDTH), lambda g: (0, 2 * groups))
    query_docs_spec = pl.BlockSpec((1, rows), lambda g: (0, 0))
    row_spec = pl.BlockSpec((1, pairs, rows), lambda g: (g, 0, 0))
    row_shape = jax.ShapeDtypeStruct((groups, pairs, rows), jnp.float32)
    tile = 2 * rows * rows * HEAD_WIDTH * heads

    def stats(block, state, own, final):
        count = 1 if final else 2
        return pl.pallas_call(
            functools.partial(stats_kernel, own, final, pairs, scale),
            grid=(groups,),
            in_specs=[pair_spec, key_spec, docs_spec, query_docs_spec, row_spec, row_spec],
            out_specs=[row_spec] * count,
            out_shape=[row_shape] * count,
            cost_estimate=pl.CostEstimate(
                flops=2 * tile, bytes_accessed=1 << 20, transcendentals=rows * rows * heads
            ),
            name="stats",
        )(query, block, block, query_docs, *state)

    state = [jnp.full(row_shape.shape, LOW, jnp.float32), jnp.zeros(row_shape.shape, jnp.float32)]
    for d in range(steps):
        state = stats(blocks[d], state, d == 0, d == steps - 1)
    log_total = state[0]

    weight = (gathered.astype(jnp.float32) * row_scale[:, None]).astype(jnp.bfloat16)
    attention_gradient = dot(grad_y, weight, LAST).astype(jnp.bfloat16)
    row_delta = jnp.sum(
        attention_gradient.reshape(rows, groups, pairs, HEAD_WIDTH).astype(jnp.float32)
        * attention_output.reshape(rows, groups, pairs, HEAD_WIDTH).astype(jnp.float32),
        axis=-1,
    ).transpose(1, 2, 0)

    def grads(block, total, own):
        first = total is None
        wide = jnp.float32 if own else jnp.bfloat16
        key_shape = jax.ShapeDtypeStruct((2, rows, groups * HEAD_WIDTH), wide)
        both_spec = pl.BlockSpec((2, rows, HEAD_WIDTH), lambda g: (0, 0, g))
        ins = [pair_spec, pair_spec, key_spec, value_spec, docs_spec, query_docs_spec]
        return pl.pallas_call(
            functools.partial(grads_kernel, own, first, pairs, scale),
            grid=(groups,),
            in_specs=ins + [row_spec, row_spec] + ([] if first else [pair_spec]),
            out_specs=[pair_spec, both_spec],
            out_shape=[
                jax.ShapeDtypeStruct(query.shape, jnp.bfloat16 if own else jnp.float32),
                key_shape,
            ],
            cost_estimate=pl.CostEstimate(
                flops=10 * tile, bytes_accessed=4 << 20, transcendentals=rows * rows * heads
            ),
            name="grads",
        )(
            query,
            attention_gradient,
            block,
            block,
            block,
            query_docs,
            log_total,
            row_delta,
            *([] if first else [total]),
        )

    total = None
    parts = []
    for d in reversed(range(steps)):
        total, part = grads(blocks[d], total, d == 0)
        if d:
            part = shift_by(part, "ctx", -d)
        parts.append(part)
    summed = sum(part.astype(jnp.float32) for part in parts).astype(jnp.bfloat16)
    key_gradient, value_gradient = summed[0], summed[1]
    grad_weight = scattered.astype(jnp.float32)
    return (total, key_gradient, value_gradient, grad_weight)


def solution(mesh):
    return jax.shard_map(
        per_device,
        mesh=mesh,
        in_specs=(
            P("ctx", "shard"),
            P("ctx", "shard"),
            P("ctx", "shard"),
            P("ctx", "shard"),
            P("ctx", None),
            P("ctx"),
            P("shard", "ctx"),
            P("shard", None, None),
            P(),
        ),
        out_specs=(P("ctx", "shard"), P("ctx", "shard"), P("ctx", "shard"), P("ctx", "shard")),
        check_vma=False,
    )
```

```python
import functools
import jax
import jax.numpy as jnp
from jax import lax
from jax.experimental import pallas as pl
from jax.experimental.pallas import tpu as pltpu
from jax.sharding import PartitionSpec as P

HEAD_WIDTH = 128
LOW = -1e30
LAST = (((1,), (1,)), ((), ()))
FIRST = (((0,), (0,)), ((), ()))
PLAIN = (((1,), (0,)), ((), ()))


def dot(a, b, dims):
    return lax.dot_general(a, b, dims, preferred_element_type=jnp.float32)


def stacked(ref, pairs):
    return jnp.concatenate(
        [ref[:, j * HEAD_WIDTH : (j + 1) * HEAD_WIDTH] for j in range(pairs)], axis=0
    )


def row_of(ref, pairs):
    return jnp.concatenate([ref[0, j : j + 1, :] for j in range(pairs)], axis=1)


def visible(key_docs_ref, query_docs_ref, pairs, own):
    key_docs = key_docs_ref[:, 0:1].astype(jnp.float32)
    query_docs = query_docs_ref[...]
    allowed = key_docs == query_docs
    if own:
        rows = query_docs.shape[1]
        n = lax.broadcasted_iota(jnp.int32, (rows, rows), 0)
        r = lax.broadcasted_iota(jnp.int32, (rows, rows), 1)
        allowed = allowed & (n <= r)
    return jnp.concatenate([allowed.astype(jnp.float32)] * pairs, axis=1) > 0.5


def stats_kernel(own, final, pairs, scale, q_ref, k_ref, kd_ref, qd_ref, m_ref, l_ref, *outs):
    rows = q_ref.shape[0]
    scores = dot(k_ref[...], stacked(q_ref, pairs), LAST) * scale
    allowed = visible(kd_ref, qd_ref, pairs, own)
    masked = jnp.where(allowed, scores, LOW)
    highest, running = row_of(m_ref, pairs), row_of(l_ref, pairs)
    newest = jnp.maximum(highest, jnp.max(masked, axis=0, keepdims=True))
    weights = jnp.where(allowed, jnp.exp(scores - newest), 0.0)
    total = running * jnp.exp(highest - newest) + jnp.sum(weights, axis=0, keepdims=True)
    results = (newest + jnp.log(total),) if final else (newest, total)
    for out, result in zip(outs, results):
        for j in range(pairs):
            out[0, j : j + 1, :] = result[:, j * rows : (j + 1) * rows]


def grads_kernel(
    own, first, pairs, scale, q_ref, a_ref, k_ref, v_ref, kd_ref, qd_ref, t_ref, d_ref, *rest
):
    if first:
        dq_ref, kv_ref = rest
    else:
        old_ref, dq_ref, kv_ref = rest
    rows = q_ref.shape[0]
    queries, grads = stacked(q_ref, pairs), stacked(a_ref, pairs)
    keys, values = k_ref[...], v_ref[...]
    scores = dot(keys, queries, LAST) * scale
    allowed = visible(kd_ref, qd_ref, pairs, own)
    attention = jnp.where(allowed, jnp.exp(scores - row_of(t_ref, pairs)), 0.0)
    attention_grad = dot(values, grads, LAST)
    score_grad = (attention * (attention_grad - row_of(d_ref, pairs))).astype(jnp.bfloat16)
    kv_ref[0] = (dot(score_grad, queries, PLAIN) * scale).astype(kv_ref.dtype)
    kv_ref[1] = dot(attention.astype(jnp.bfloat16), grads, PLAIN).astype(kv_ref.dtype)
    query_add = dot(score_grad, keys, FIRST) * scale
    for j in range(pairs):
        part = query_add[j * rows : (j + 1) * rows, :]
        cols = slice(j * HEAD_WIDTH, (j + 1) * HEAD_WIDTH)
        if not first:
            part = part + old_ref[:, cols]
        dq_ref[:, cols] = part.astype(dq_ref.dtype)


def gather_orders(count):
    bits = count.bit_length() - 1
    top, middle = [bits - 1, bits - 2], list(range(bits - 3, 0, -1))
    return (top + middle + [0], middle + top + [0])


def gather_kernel(count, code_ref, out_ref, send_sem, recv_sem):
    me = lax.axis_index("ctx")
    bits = count.bit_length() - 1
    half = code_ref.shape[0] // 2
    step = [(1 - 2 * ((me // (1 << b)) % 2)) * (1 << b) for b in range(bits)]

    def moved(mask):
        return me + sum(step[b] for b in range(bits) if mask >> b & 1)

    barrier = pltpu.get_barrier_semaphore()
    for b in range(bits):
        pl.semaphore_signal(
            barrier,
            inc=1,
            device_id={"ctx": moved(1 << b)},
            device_id_type=pl.DeviceIdType.MESH,
        )
    pl.semaphore_wait(barrier, bits)

    def transfer(part, mask, bit):
        rows = pl.ds(part * half, half)
        source = code_ref.at[rows] if mask == 0 else out_ref.at[moved(mask), rows]
        slot = part * count + (mask | 1 << bit)
        return pltpu.make_async_remote_copy(
            src_ref=source,
            dst_ref=out_ref.at[moved(mask), rows],
            send_sem=send_sem.at[slot],
            recv_sem=recv_sem.at[slot],
            device_id={"ctx": moved(1 << bit)},
            device_id_type=pl.DeviceIdType.MESH,
        )

    orders = gather_orders(count)
    held = [[0], [0]]
    started = []
    arrived = [{}, {}]
    for stage in range(bits):
        for part in range(2):
            bit = orders[part][stage]
            new = []
            for mask in held[part]:
                if mask in arrived[part]:
                    arrived[part].pop(mask).wait_recv()
                copy = transfer(part, mask, bit)
                copy.start()
                started.append(copy)
                new.append(mask | 1 << bit)
                arrived[part][mask | 1 << bit] = copy
            held[part] = held[part] + new
        if stage == 0:
            out_ref[me] = code_ref[...]
    for part in range(2):
        for copy in arrived[part].values():
            copy.wait_recv()
    for copy in started:
        copy.wait_send()


def gather(codes, count):
    return pl.pallas_call(
        functools.partial(gather_kernel, count),
        out_shape=jax.ShapeDtypeStruct((count, *codes.shape), codes.dtype),
        in_specs=[pl.BlockSpec(memory_space=pltpu.VMEM)],
        out_specs=pl.BlockSpec(memory_space=pltpu.VMEM),
        scratch_shapes=[pltpu.SemaphoreType.DMA((2 * count,))] * 2,
        compiler_params=pltpu.CompilerParams(collective_id=0, has_side_effects=True),
        cost_estimate=pl.CostEstimate(flops=0, bytes_accessed=100 << 20, transcendentals=0),
        name="gather",
    )(codes)


def project_kernel(pairs, y_ref, code_ref, scale_ref, o_ref, a_ref, d_ref):
    scales = scale_ref[...]
    weight = jnp.concatenate(
        [
            (code_ref[c].astype(jnp.float32) * scales).astype(jnp.bfloat16)
            for c in range(code_ref.shape[0])
        ],
        axis=1,
    )
    grads = dot(y_ref[...], weight, LAST).astype(jnp.bfloat16)
    a_ref[...] = grads
    product = grads.astype(jnp.float32) * o_ref[...].astype(jnp.float32)
    for j in range(pairs):
        cols = slice(j * HEAD_WIDTH, (j + 1) * HEAD_WIDTH)
        d_ref[0, j : j + 1, :] = jnp.sum(product[:, cols].T, axis=0, keepdims=True)


def plane_turn(x, plane, by):
    size = lax.axis_size("ctx")
    return lax.ppermute(
        x, "ctx", [(i, i // plane * plane + (i % plane + by) % plane) for i in range(size)]
    )


def shift_by(x, axis, by):
    size = lax.axis_size(axis)
    return lax.ppermute(x, axis, [(i, i + by) for i in range(size) if 0 <= i + by < size])


def per_device(query, key, value, attention_output, grad_y, doc_ids, codes, scale_copies, holder):
    rows = query.shape[0]
    heads = query.shape[1] // HEAD_WIDTH
    groups = key.shape[1] // HEAD_WIDTH
    pairs = heads // groups
    shard_index = lax.axis_index("shard")
    shards = lax.axis_size("shard")
    ctx_count = lax.axis_size("ctx")
    steps = ctx_count // 4 + 1
    scale = HEAD_WIDTH ** (-0.5)

    ctx_index = lax.axis_index("ctx")
    plane = steps - 1
    place = ctx_index % plane
    bits = ctx_count.bit_length() - 1

    gathered = gather(codes, ctx_count)

    docs = (doc_ids + 1).astype(jnp.bfloat16)
    packed = jnp.concatenate(
        [key, value, jnp.broadcast_to(docs[:, None], (rows, HEAD_WIDTH))], axis=1
    )
    query_docs = (doc_ids + 1).astype(jnp.float32)[None, :]
    before = shift_by(packed, "ctx", plane)
    blocks = [packed]
    for d in range(1, plane):
        blocks.append(plane_turn(jnp.where(place + d < plane, packed, before), plane, d))
    blocks.append(before)

    masked_table = jnp.where((holder == shard_index)[:, None], scale_copies[0], 0.0)
    scale_table = masked_table
    for i in range(1, shards):
        scale_table = scale_table + lax.ppermute(
            masked_table, "shard", [(j, (j + i) % shards) for j in range(shards)]
        )
    row_scale = lax.dynamic_slice_in_dim(scale_table, shard_index * heads, heads, 0).reshape(
        heads * HEAD_WIDTH
    )

    columns = attention_output.shape[1]
    summed_weight = dot(grad_y, attention_output, FIRST) * (rows * ctx_count) ** (-0.5)
    summed_weight = summed_weight.reshape(ctx_count, -1, columns)
    left = list(range(bits))
    for bit in [0] + list(range(1, bits)):
        shape = summed_weight.shape
        low = 1 << left.index(bit)
        left.remove(bit)
        split = summed_weight.reshape(shape[0] // (2 * low), 2, low, *shape[1:])
        mine = (ctx_index // (1 << bit)) % 2
        kept = lax.dynamic_index_in_dim(split, mine, 1, keepdims=False)
        sent = lax.dynamic_index_in_dim(split, 1 - mine, 1, keepdims=False).astype(jnp.bfloat16)
        got = lax.ppermute(sent, "ctx", [(i, i ^ (1 << bit)) for i in range(ctx_count)])
        summed_weight = (kept + got.astype(jnp.float32)).reshape(shape[0] // 2, *shape[1:])
    grad_weight = summed_weight[0]

    pair_spec = pl.BlockSpec((rows, pairs * HEAD_WIDTH), lambda g: (0, g))
    key_spec = pl.BlockSpec((rows, HEAD_WIDTH), lambda g: (0, g))
    value_spec = pl.BlockSpec((rows, HEAD_WIDTH), lambda g: (0, groups + g))
    docs_spec = pl.BlockSpec((rows, HEAD_WIDTH), lambda g: (0, 2 * groups))
    query_docs_spec = pl.BlockSpec((1, rows), lambda g: (0, 0))
    row_spec = pl.BlockSpec((1, pairs, rows), lambda g: (g, 0, 0))
    row_shape = jax.ShapeDtypeStruct((groups, pairs, rows), jnp.float32)
    tile = 2 * rows * rows * HEAD_WIDTH * heads

    def stats(block, state, own, final):
        count = 1 if final else 2
        return pl.pallas_call(
            functools.partial(stats_kernel, own, final, pairs, scale),
            grid=(groups,),
            in_specs=[pair_spec, key_spec, docs_spec, query_docs_spec, row_spec, row_spec],
            out_specs=[row_spec] * count,
            out_shape=[row_shape] * count,
            cost_estimate=pl.CostEstimate(
                flops=2 * tile, bytes_accessed=1 << 20, transcendentals=rows * rows * heads
            ),
            name="stats",
        )(query, block, block, query_docs, *state)

    state = [jnp.full(row_shape.shape, LOW, jnp.float32), jnp.zeros(row_shape.shape, jnp.float32)]
    for d in range(steps):
        state = stats(blocks[d], state, d == 0, d == steps - 1)
    log_total = state[0]

    if codes.shape[1] % HEAD_WIDTH == 0:
        attention_gradient, row_delta = pl.pallas_call(
            functools.partial(project_kernel, pairs),
            grid=(groups,),
            in_specs=[
                pl.BlockSpec(grad_y.shape, lambda g: (0, 0)),
                pl.BlockSpec((ctx_count, pairs * HEAD_WIDTH, codes.shape[1]), lambda g: (0, g, 0)),
                pl.BlockSpec((pairs * HEAD_WIDTH, 1), lambda g: (g, 0)),
                pair_spec,
            ],
            out_specs=[pair_spec, row_spec],
            out_shape=[jax.ShapeDtypeStruct(query.shape, jnp.bfloat16), row_shape],
            cost_estimate=pl.CostEstimate(
                flops=2 * rows * grad_y.shape[1] * query.shape[1],
                bytes_accessed=6 << 20,
                transcendentals=0,
            ),
            name="project",
        )(grad_y, gathered, row_scale[:, None], attention_output)
    else:
        weight = (gathered.astype(jnp.float32) * row_scale[None, :, None]).astype(jnp.bfloat16)
        weight = weight.transpose(1, 0, 2).reshape(codes.shape[0], -1)
        attention_gradient = dot(grad_y, weight, LAST).astype(jnp.bfloat16)
        row_delta = jnp.sum(
            attention_gradient.reshape(rows, groups, pairs, HEAD_WIDTH).astype(jnp.float32)
            * attention_output.reshape(rows, groups, pairs, HEAD_WIDTH).astype(jnp.float32),
            axis=-1,
        ).transpose(1, 2, 0)

    def grads(block, total, own):
        first = total is None
        wide = jnp.float32 if own else jnp.bfloat16
        key_shape = jax.ShapeDtypeStruct((2, rows, groups * HEAD_WIDTH), wide)
        both_spec = pl.BlockSpec((2, rows, HEAD_WIDTH), lambda g: (0, 0, g))
        ins = [pair_spec, pair_spec, key_spec, value_spec, docs_spec, query_docs_spec]
        return pl.pallas_call(
            functools.partial(grads_kernel, own, first, pairs, scale),
            grid=(groups,),
            in_specs=ins + [row_spec, row_spec] + ([] if first else [pair_spec]),
            out_specs=[pair_spec, both_spec],
            out_shape=[
                jax.ShapeDtypeStruct(query.shape, jnp.bfloat16 if own else jnp.float32),
                key_shape,
            ],
            cost_estimate=pl.CostEstimate(
                flops=10 * tile, bytes_accessed=4 << 20, transcendentals=rows * rows * heads
            ),
            name="grads",
        )(
            query,
            attention_gradient,
            block,
            block,
            block,
            query_docs,
            log_total,
            row_delta,
            *([] if first else [total]),
        )

    total = None
    turned = {}
    for d in grads_order(plane):
        total, part = grads(blocks[d], total, d == 0)
        if d == plane:
            far = part
        elif d == 0:
            near = part
        else:
            turned[d] = plane_turn(part, plane, -d)
    wrapped = far.astype(jnp.float32)
    for d in range(1, plane):
        wrapped = wrapped + jnp.where(place + d >= plane, turned[d].astype(jnp.float32), 0.0)
    wrapped = shift_by(wrapped.astype(jnp.bfloat16), "ctx", -plane)
    for d in range(1, plane):
        near = near + jnp.where(place + d < plane, turned[d].astype(jnp.float32), 0.0)
    summed = (near + wrapped.astype(jnp.float32)).astype(jnp.bfloat16)
    key_gradient, value_gradient = summed[0], summed[1]
    return (total, key_gradient, value_gradient, grad_weight)


def grads_order(plane):
    inner = list(range(1, plane))
    inner.sort(key=lambda d: abs(2 * d - plane))
    return inner + [plane, 0]


def solution(mesh):
    return jax.shard_map(
        per_device,
        mesh=mesh,
        in_specs=(
            P("ctx", "shard"),
            P("ctx", "shard"),
            P("ctx", "shard"),
            P("ctx", "shard"),
            P("ctx", None),
            P("ctx"),
            P("shard", "ctx"),
            P("shard", None, None),
            P(),
        ),
        out_specs=(P("ctx", "shard"), P("ctx", "shard"), P("ctx", "shard"), P("ctx", "shard")),
        check_vma=False,
    )
```

```python
import functools
import jax
import jax.numpy as jnp
from jax import lax
from jax.experimental import pallas as pl
from jax.experimental.pallas import tpu as pltpu
from jax.sharding import PartitionSpec as P

HEAD_WIDTH = 128
LOW = -1e30
LAST = (((1,), (1,)), ((), ()))
FIRST = (((0,), (0,)), ((), ()))
PLAIN = (((1,), (0,)), ((), ()))


def dot(a, b, dims):
    return lax.dot_general(a, b, dims, preferred_element_type=jnp.float32)


def stacked(ref, pairs):
    return jnp.concatenate(
        [ref[:, j * HEAD_WIDTH : (j + 1) * HEAD_WIDTH] for j in range(pairs)], axis=0
    )


def row_of(ref, pairs):
    return jnp.concatenate([ref[0, j : j + 1, :] for j in range(pairs)], axis=1)


def visible(key_docs_ref, query_docs_ref, pairs, own):
    key_docs = key_docs_ref[:, 0:1].astype(jnp.float32)
    query_docs = query_docs_ref[...]
    allowed = key_docs == query_docs
    if own:
        rows = query_docs.shape[1]
        n = lax.broadcasted_iota(jnp.int32, (rows, rows), 0)
        r = lax.broadcasted_iota(jnp.int32, (rows, rows), 1)
        allowed = allowed & (n <= r)
    return jnp.concatenate([allowed.astype(jnp.float32)] * pairs, axis=1) > 0.5


def stats_kernel(owns, final, pairs, scale, q_ref, *refs):
    count = len(owns)
    blocks = refs[: 2 * count]
    qd_ref, m_ref, l_ref, *outs = refs[2 * count :]
    rows = q_ref.shape[0]
    queries = stacked(q_ref, pairs)
    masked = [
        jnp.where(
            visible(blocks[2 * i + 1], qd_ref, pairs, owns[i]),
            dot(blocks[2 * i][...], queries, LAST) * scale,
            LOW,
        )
        for i in range(count)
    ]
    highest, running = row_of(m_ref, pairs), row_of(l_ref, pairs)
    newest = highest
    for scores in masked:
        newest = jnp.maximum(newest, jnp.max(scores, axis=0, keepdims=True))
    total = running * jnp.exp(highest - newest)
    for scores in masked:
        total = total + jnp.sum(jnp.exp(scores - newest), axis=0, keepdims=True)
    results = (newest + jnp.log(total),) if final else (newest, total)
    for out, result in zip(outs, results):
        for j in range(pairs):
            out[0, j : j + 1, :] = result[:, j * rows : (j + 1) * rows]


def grads_kernel(
    own, first, pairs, scale, q_ref, a_ref, k_ref, v_ref, kd_ref, qd_ref, t_ref, d_ref, *rest
):
    if first:
        dq_ref, kv_ref = rest
    else:
        old_ref, dq_ref, kv_ref = rest
    rows = q_ref.shape[0]
    queries, grads = stacked(q_ref, pairs), stacked(a_ref, pairs)
    keys, values = k_ref[...], v_ref[...]
    scores = dot(keys, queries, LAST) * scale
    allowed = visible(kd_ref, qd_ref, pairs, own)
    attention = jnp.where(allowed, jnp.exp(scores - row_of(t_ref, pairs)), 0.0)
    attention_grad = dot(values, grads, LAST)
    score_grad = (attention * (attention_grad - row_of(d_ref, pairs))).astype(jnp.bfloat16)
    kv_ref[0] = (dot(score_grad, queries, PLAIN) * scale).astype(kv_ref.dtype)
    kv_ref[1] = dot(attention.astype(jnp.bfloat16), grads, PLAIN).astype(kv_ref.dtype)
    query_add = dot(score_grad, keys, FIRST) * scale
    for j in range(pairs):
        part = query_add[j * rows : (j + 1) * rows, :]
        cols = slice(j * HEAD_WIDTH, (j + 1) * HEAD_WIDTH)
        if not first:
            part = part + old_ref[:, cols]
        dq_ref[:, cols] = part.astype(dq_ref.dtype)


def gather_orders(count):
    bits = count.bit_length() - 1
    top, middle = [bits - 1, bits - 2], list(range(bits - 3, 0, -1))
    return (top + middle + [0], middle + top + [0])


def gather_kernel(count, code_ref, out_ref, send_sem, recv_sem):
    me = lax.axis_index("ctx")
    bits = count.bit_length() - 1
    half = code_ref.shape[0] // 2
    step = [(1 - 2 * ((me // (1 << b)) % 2)) * (1 << b) for b in range(bits)]

    def moved(mask):
        return me + sum(step[b] for b in range(bits) if mask >> b & 1)

    barrier = pltpu.get_barrier_semaphore()
    for b in range(bits):
        pl.semaphore_signal(
            barrier,
            inc=1,
            device_id={"ctx": moved(1 << b)},
            device_id_type=pl.DeviceIdType.MESH,
        )
    pl.semaphore_wait(barrier, bits)

    def transfer(part, mask, bit):
        rows = pl.ds(part * half, half)
        source = code_ref.at[rows] if mask == 0 else out_ref.at[moved(mask), rows]
        slot = part * count + (mask | 1 << bit)
        return pltpu.make_async_remote_copy(
            src_ref=source,
            dst_ref=out_ref.at[moved(mask), rows],
            send_sem=send_sem.at[slot],
            recv_sem=recv_sem.at[slot],
            device_id={"ctx": moved(1 << bit)},
            device_id_type=pl.DeviceIdType.MESH,
        )

    orders = gather_orders(count)
    held = [[0], [0]]
    started = []
    arrived = [{}, {}]
    for stage in range(bits):
        for part in range(2):
            bit = orders[part][stage]
            new = []
            for mask in held[part]:
                if mask in arrived[part]:
                    arrived[part].pop(mask).wait_recv()
                copy = transfer(part, mask, bit)
                copy.start()
                started.append(copy)
                new.append(mask | 1 << bit)
                arrived[part][mask | 1 << bit] = copy
            held[part] = held[part] + new
        if stage == 0:
            out_ref[me] = code_ref[...]
    for part in range(2):
        for copy in arrived[part].values():
            copy.wait_recv()
    for copy in started:
        copy.wait_send()


def gather(codes, count):
    return pl.pallas_call(
        functools.partial(gather_kernel, count),
        out_shape=jax.ShapeDtypeStruct((count, *codes.shape), codes.dtype),
        in_specs=[pl.BlockSpec(memory_space=pltpu.VMEM)],
        out_specs=pl.BlockSpec(memory_space=pltpu.VMEM),
        scratch_shapes=[pltpu.SemaphoreType.DMA((2 * count,))] * 2,
        compiler_params=pltpu.CompilerParams(collective_id=0, has_side_effects=True),
        cost_estimate=pl.CostEstimate(flops=0, bytes_accessed=100 << 20, transcendentals=0),
        name="gather",
    )(codes)


def project_kernel(pairs, y_ref, code_ref, scale_ref, o_ref, a_ref, d_ref):
    scales = scale_ref[...]
    weight = jnp.concatenate(
        [
            (code_ref[c].astype(jnp.float32) * scales).astype(jnp.bfloat16)
            for c in range(code_ref.shape[0])
        ],
        axis=1,
    )
    grads = dot(y_ref[...], weight, LAST).astype(jnp.bfloat16)
    a_ref[...] = grads
    product = grads.astype(jnp.float32) * o_ref[...].astype(jnp.float32)
    for j in range(pairs):
        cols = slice(j * HEAD_WIDTH, (j + 1) * HEAD_WIDTH)
        d_ref[0, j : j + 1, :] = jnp.sum(product[:, cols].T, axis=0, keepdims=True)


def plane_turn(x, plane, by):
    size = lax.axis_size("ctx")
    return lax.ppermute(
        x, "ctx", [(i, i // plane * plane + (i % plane + by) % plane) for i in range(size)]
    )


def shift_by(x, axis, by):
    size = lax.axis_size(axis)
    return lax.ppermute(x, axis, [(i, i + by) for i in range(size) if 0 <= i + by < size])


def per_device(query, key, value, attention_output, grad_y, doc_ids, codes, scale_copies, holder):
    rows = query.shape[0]
    heads = query.shape[1] // HEAD_WIDTH
    groups = key.shape[1] // HEAD_WIDTH
    pairs = heads // groups
    shard_index = lax.axis_index("shard")
    shards = lax.axis_size("shard")
    ctx_count = lax.axis_size("ctx")
    steps = ctx_count // 4 + 1
    scale = HEAD_WIDTH ** (-0.5)

    ctx_index = lax.axis_index("ctx")
    plane = steps - 1
    place = ctx_index % plane
    bits = ctx_count.bit_length() - 1

    gathered = gather(codes, ctx_count)

    docs = (doc_ids + 1).astype(jnp.bfloat16)
    packed = jnp.concatenate(
        [key, value, jnp.broadcast_to(docs[:, None], (rows, HEAD_WIDTH))], axis=1
    )
    query_docs = (doc_ids + 1).astype(jnp.float32)[None, :]
    before = shift_by(packed, "ctx", plane)
    blocks = [packed]
    for d in range(1, plane):
        blocks.append(plane_turn(jnp.where(place + d < plane, packed, before), plane, d))
    blocks.append(before)

    masked_table = jnp.where((holder == shard_index)[:, None], scale_copies[0], 0.0)
    scale_table = masked_table
    for i in range(1, shards):
        scale_table = scale_table + lax.ppermute(
            masked_table, "shard", [(j, (j + i) % shards) for j in range(shards)]
        )
    row_scale = lax.dynamic_slice_in_dim(scale_table, shard_index * heads, heads, 0).reshape(
        heads * HEAD_WIDTH
    )

    columns = attention_output.shape[1]
    summed_weight = (
        dot(grad_y, attention_output, FIRST) * (rows * ctx_count) ** (-0.5)
    ).astype(jnp.bfloat16)
    summed_weight = summed_weight.reshape(ctx_count, -1, columns)
    left = list(range(bits))
    for bit in range(bits):
        shape = summed_weight.shape
        low = 1 << left.index(bit)
        left.remove(bit)
        split = summed_weight.reshape(shape[0] // (2 * low), 2, low, *shape[1:])
        mine = (ctx_index // (1 << bit)) % 2
        kept = lax.dynamic_index_in_dim(split, mine, 1, keepdims=False)
        sent = lax.dynamic_index_in_dim(split, 1 - mine, 1, keepdims=False).astype(jnp.bfloat16)
        got = lax.ppermute(sent, "ctx", [(i, i ^ (1 << bit)) for i in range(ctx_count)])
        summed_weight = (kept.astype(jnp.float32) + got.astype(jnp.float32)).reshape(shape[0] // 2, *shape[1:])
    grad_weight = summed_weight[0]

    pair_spec = pl.BlockSpec((rows, pairs * HEAD_WIDTH), lambda g: (0, g))
    key_spec = pl.BlockSpec((rows, HEAD_WIDTH), lambda g: (0, g))
    value_spec = pl.BlockSpec((rows, HEAD_WIDTH), lambda g: (0, groups + g))
    docs_spec = pl.BlockSpec((rows, HEAD_WIDTH), lambda g: (0, 2 * groups))
    query_docs_spec = pl.BlockSpec((1, rows), lambda g: (0, 0))
    row_spec = pl.BlockSpec((1, pairs, rows), lambda g: (g, 0, 0))
    row_shape = jax.ShapeDtypeStruct((groups, pairs, rows), jnp.float32)
    tile = 2 * rows * rows * HEAD_WIDTH * heads

    def stats(chunk, state, owns, final):
        count = 1 if final else 2
        return pl.pallas_call(
            functools.partial(stats_kernel, owns, final, pairs, scale),
            grid=(groups,),
            in_specs=[pair_spec]
            + [key_spec, docs_spec] * len(chunk)
            + [query_docs_spec, row_spec, row_spec],
            out_specs=[row_spec] * count,
            out_shape=[row_shape] * count,
            cost_estimate=pl.CostEstimate(
                flops=2 * tile * len(chunk),
                bytes_accessed=len(chunk) << 20,
                transcendentals=rows * rows * heads * len(chunk),
            ),
            name="stats",
        )(query, *[block for block in chunk for _ in range(2)], query_docs, *state)

    state = [jnp.full(row_shape.shape, LOW, jnp.float32), jnp.zeros(row_shape.shape, jnp.float32)]
    state = stats(blocks[:1], state, (True,), False)
    for start in range(1, steps, 4):
        chunk = blocks[start : start + 4]
        state = stats(chunk, state, (False,) * len(chunk), start + 4 >= steps)
    log_total = state[0]

    if codes.shape[1] % HEAD_WIDTH == 0:
        attention_gradient, row_delta = pl.pallas_call(
            functools.partial(project_kernel, pairs),
            grid=(groups,),
            in_specs=[
                pl.BlockSpec(grad_y.shape, lambda g: (0, 0)),
                pl.BlockSpec((ctx_count, pairs * HEAD_WIDTH, codes.shape[1]), lambda g: (0, g, 0)),
                pl.BlockSpec((pairs * HEAD_WIDTH, 1), lambda g: (g, 0)),
                pair_spec,
            ],
            out_specs=[pair_spec, row_spec],
            out_shape=[jax.ShapeDtypeStruct(query.shape, jnp.bfloat16), row_shape],
            cost_estimate=pl.CostEstimate(
                flops=2 * rows * grad_y.shape[1] * query.shape[1],
                bytes_accessed=6 << 20,
                transcendentals=0,
            ),
            name="project",
        )(grad_y, gathered, row_scale[:, None], attention_output)
    else:
        weight = (gathered.astype(jnp.float32) * row_scale[None, :, None]).astype(jnp.bfloat16)
        weight = weight.transpose(1, 0, 2).reshape(codes.shape[0], -1)
        attention_gradient = dot(grad_y, weight, LAST).astype(jnp.bfloat16)
        row_delta = jnp.sum(
            attention_gradient.reshape(rows, groups, pairs, HEAD_WIDTH).astype(jnp.float32)
            * attention_output.reshape(rows, groups, pairs, HEAD_WIDTH).astype(jnp.float32),
            axis=-1,
        ).transpose(1, 2, 0)

    def grads(block, total, own):
        first = total is None
        wide = jnp.float32 if own else jnp.bfloat16
        key_shape = jax.ShapeDtypeStruct((2, rows, groups * HEAD_WIDTH), wide)
        both_spec = pl.BlockSpec((2, rows, HEAD_WIDTH), lambda g: (0, 0, g))
        ins = [pair_spec, pair_spec, key_spec, value_spec, docs_spec, query_docs_spec]
        return pl.pallas_call(
            functools.partial(grads_kernel, own, first, pairs, scale),
            grid=(groups,),
            in_specs=ins + [row_spec, row_spec] + ([] if first else [pair_spec]),
            out_specs=[pair_spec, both_spec],
            out_shape=[
                jax.ShapeDtypeStruct(query.shape, jnp.bfloat16 if own else jnp.float32),
                key_shape,
            ],
            cost_estimate=pl.CostEstimate(
                flops=10 * tile, bytes_accessed=4 << 20, transcendentals=rows * rows * heads
            ),
            name="grads",
        )(
            query,
            attention_gradient,
            block,
            block,
            block,
            query_docs,
            log_total,
            row_delta,
            *([] if first else [total]),
        )

    total = None
    turned = {}
    for d in grads_order(plane):
        total, part = grads(blocks[d], total, d == 0)
        if d == plane:
            far = part
        elif d == 0:
            near = part
        else:
            turned[d] = plane_turn(part, plane, -d)
    wrapped = far.astype(jnp.float32)
    for d in range(1, plane):
        wrapped = wrapped + jnp.where(place + d >= plane, turned[d].astype(jnp.float32), 0.0)
    wrapped = shift_by(wrapped.astype(jnp.bfloat16), "ctx", -plane)
    for d in range(1, plane):
        near = near + jnp.where(place + d < plane, turned[d].astype(jnp.float32), 0.0)
    summed = (near + wrapped.astype(jnp.float32)).astype(jnp.bfloat16)
    key_gradient, value_gradient = summed[0], summed[1]
    return (total, key_gradient, value_gradient, grad_weight)


def grads_order(plane):
    inner = list(range(1, plane))
    inner.sort(key=lambda d: abs(2 * d - plane))
    return inner + [plane, 0]


def solution(mesh):
    return jax.shard_map(
        per_device,
        mesh=mesh,
        in_specs=(
            P("ctx", "shard"),
            P("ctx", "shard"),
            P("ctx", "shard"),
            P("ctx", "shard"),
            P("ctx", None),
            P("ctx"),
            P("shard", "ctx"),
            P("shard", None, None),
            P(),
        ),
        out_specs=(P("ctx", "shard"), P("ctx", "shard"), P("ctx", "shard"), P("ctx", "shard")),
        check_vma=False,
    )
```
